32 devices in a mesh: row: 4 (over y, core), feat: 8 (over z, x).
Axes of the slice: x: 2, y: 2, z: 4, core: 2. Of those that a mesh axis runs over, the one named last changes fastest.
Arguments:
- codes: int32 [4096, 2048], P('row', 'feat'), may hold values from 0 to 255
- node_ids: int32 [4096], P('row'), may hold values from 0 to 31
- grads: bfloat16 [4096], P('row'), may hold values from -6 to 6
- hessians: bfloat16 [4096], P('row'), may hold values from 0.099609375 to 1
- split_feature: int32 [32], replicated, may hold values from 0 to 2047
- threshold: int32 [32], replicated, may hold values from 0 to 254
Outputs:
- gains: float32 [2048, 64, 256], P(('feat', 'row'))
The draws below stay inside these ranges and needn't reach their ends.
Inputs may be any that keep to these rules, and one draw needn't show every extreme that they name: `codes`: codes are small integers, and a program may move them packed several to a 32-bit word.
All inputs are finite; a program needn't handle non-finite values.
Results may differ from the reference program's by a relative error of at most 0.0003.
Values may be sent and summed in bfloat16 or wider, within the bound.
A program may use at most 64 MiB of HBM per device.

```python
import math
import jax
import jax.numpy as jnp
from jax import lax

FEATS = 2048
BINS = 256
PARENTS = 32
ROWS = 4096


def with_ends(array, rng, low, largest):
    dims = array.shape
    place = [jax.random.randint(jax.random.fold_in(rng, axis), (), 0, dims[axis]) for axis in range(len(dims))]
    array = array.at[tuple(place)].set(low)
    longest = dims.index(max(dims))
    place[longest] = (place[longest] + 1) % dims[longest]
    return array.at[tuple(place)].set(largest)


def levels(own_key, extent, split, smallest, high):
    def one(position, parts):
        steps = jax.random.uniform(jax.random.fold_in(jax.random.fold_in(own_key, 6), position), (parts,), jnp.float32, smallest / len(split), high / len(split))
        return jnp.repeat(jnp.exp(steps), extent[position] // parts).reshape((-1,) + (1,) * (len(extent) - position - 1))

    loudness = one(*split[0])
    for cut in split[1:]:
        loudness = loudness * one(*cut)
    return loudness


def noise(own_key, extent, scale, bound, split=(), held_as=jnp.bfloat16):
    gain = levels(own_key, extent, split, -0.22, 0.18) if split else 1.0
    entries = jax.random.normal(own_key, extent, jnp.float32) * scale * gain
    return jnp.minimum(jnp.maximum(entries, -bound), bound).astype(held_as)


def setup_inputs(seed: int = 0) -> dict:
    keys = jax.random.split(jax.random.key(seed), 7)
    return {
        "codes": with_ends(jax.random.randint(keys[0], (ROWS, FEATS), 0, BINS), jax.random.fold_in(keys[0], 1), 0, BINS - 1).astype(jnp.int32),
        "node_ids": with_ends(jax.random.randint(keys[1], (ROWS,), 0, PARENTS), jax.random.fold_in(keys[1], 1), 0, PARENTS - 1).astype(jnp.int32),
        "grads": noise(keys[2], (ROWS,), 1.0, 6.0, ((0, 4),)),
        "hessians": jnp.clip(jnp.exp(math.log(1.0) - 2.306499 * jax.random.uniform(keys[3], (ROWS,), jnp.float32) ** levels(keys[3], (ROWS,), ((0, 4),), -0.2, 0.2)), 0.099609375, 1.0).astype(jnp.bfloat16),
        "split_feature": with_ends(jax.random.randint(keys[4], (PARENTS,), 0, FEATS), jax.random.fold_in(keys[4], 1), 0, FEATS - 1).astype(jnp.int32),
        "threshold": with_ends(jax.random.randint(keys[5], (PARENTS,), 0, BINS - 1), jax.random.fold_in(keys[5], 1), 0, (BINS - 1) - 1).astype(jnp.int32),
    }


def split_gains(hist):
    nodes = hist.shape[2] // 2
    width = hist.shape[1]
    across = jnp.arange(width)
    lower = (across[:, None] >= across[None, :]).astype(jnp.float32)
    left = jnp.einsum("cb,fbk->fck", lower, hist, precision=lax.Precision.HIGHEST)
    total = left[:, -1:, :]
    right = total - left
    grad_left, hess_left = left[:, :, :nodes], left[:, :, nodes:]
    grad_right, hess_right = right[:, :, :nodes], right[:, :, nodes:]
    grad_all, hess_all = total[:, :, :nodes], total[:, :, nodes:]
    value = grad_left * grad_left / (hess_left + 1.0) + grad_right * grad_right / (hess_right + 1.0)
    value = 0.5 * (value - grad_all * grad_all / (hess_all + 1.0))
    return jnp.transpose(value, (0, 2, 1))


def reference(codes, node_ids, grads, hessians, split_feature, threshold):
    rows = codes.shape[0]
    feature_row = split_feature[node_ids]
    picked = codes[jnp.arange(rows), feature_row]
    bit = (picked > threshold[node_ids]).astype(jnp.int32)
    child = 2 * node_ids + bit
    nodes = 2 * PARENTS
    member = child[:, None] == jnp.arange(nodes, dtype=jnp.int32)[None, :]
    zero = jnp.zeros((), jnp.bfloat16)
    weighted = jnp.concatenate([jnp.where(member, grads[:, None], zero), jnp.where(member, hessians[:, None], zero)], axis=1)
    weighted = weighted.astype(jnp.float32)

    def one_feature(column):
        return jax.ops.segment_sum(weighted, column, num_segments=BINS)

    hist = lax.map(one_feature, jnp.transpose(codes))
    return split_gains(hist)
```

```python
import functools

import jax
import jax.numpy as jnp
from jax import lax
from jax.experimental import pallas as pl
from jax.experimental.pallas import tpu as pltpu
from jax.sharding import PartitionSpec as P

BINS = 256
GROUP = 16
MESH = pl.DeviceIdType.MESH
NT = (((1,), (1,)), ((), ()))
F32, BF16, FLAG = jnp.float32, jnp.bfloat16, jnp.float8_e4m3fn


def largest_divisor(number, limit):
    return max(d for d in range(1, limit + 1) if number % d == 0)


def as_row(block):
    return jnp.concatenate([block[i : i + 1] for i in range(block.shape[0])], axis=1)


def weigh(w, meta, slot, start):
    nodes, rows = w.shape[0] // 2, meta.shape[2]
    number = lax.broadcasted_iota(jnp.int32, (nodes, rows), 0).astype(F32)
    member = meta[slot, 0:1, :] == number
    w[0:nodes, start : start + rows] = jnp.where(member, meta[slot, 1:2, :], 0.0).astype(BF16)
    w[nodes:, start : start + rows] = jnp.where(member, meta[slot, 2:3, :], 0.0).astype(BF16)


def below(codes32, feature, start, width):
    code = codes32[pl.ds(feature, 1), pl.ds(start, width)].astype(BF16)
    bins = lax.broadcasted_iota(jnp.int32, (BINS, width), 0).astype(F32).astype(BF16)
    one, zero = jnp.ones((), FLAG), jnp.zeros((), FLAG)
    return jnp.where(bins >= code, one, zero)


def left_sums(w, codes32, feature, start, width):
    return lax.dot_general(
        w[:, pl.ds(start, width)], below(codes32, feature, start, width), NT,
        preferred_element_type=F32,
    )


def gather_kernel(
    nr, nf, sf_hbm, thr_hbm, codes_hbm, node_hbm, grad_hbm, hess_hbm,
    acc, codes_out, w_out,
    sf_ref, thr_ref, codes_vm, node_vm, grad_vm, hess_vm,
    codes_t, codes_in, codes32, flags, meta, w,
    load_sem, flag_send, flag_recv, code_send, code_recv, meta_send, meta_recv,
):
    rows, feat_dev = codes_vm.shape
    feats = feat_dev // nr
    parents = sf_ref.shape[0]
    nodes = 2 * parents
    my_row, my_feat = lax.axis_index("row"), lax.axis_index("feat")
    group = largest_divisor(feats, GROUP)

    loads = []
    for i, (source, target) in enumerate(
        (
            (codes_hbm, codes_vm), (sf_hbm, sf_ref), (thr_hbm, thr_ref),
            (node_hbm, node_vm), (grad_hbm, grad_vm), (hess_hbm, hess_vm),
        )
    ):
        load = pltpu.make_async_copy(source, target, load_sem.at[i])
        load.start()
        loads.append(load)
    barrier = pltpu.get_barrier_semaphore()
    for t in range(1, nf):
        pl.semaphore_signal(
            barrier, inc=1, device_id={"feat": lax.rem(my_feat + t, nf)}, device_id_type=MESH
        )
    for t in range(1, nr):
        pl.semaphore_signal(
            barrier, inc=1, device_id={"row": lax.rem(my_row + t, nr)}, device_id_type=MESH
        )

    for load in loads[1:]:
        load.wait()
    parent = lax.broadcasted_iota(jnp.int32, (parents, feat_dev), 0)
    split = jnp.zeros((parents, feat_dev), jnp.int32)
    limit = jnp.zeros((parents, 128), jnp.int32)
    for p in range(parents):
        split = jnp.where(parent == p, sf_ref[p], split)
        limit = jnp.where(parent[:, :128] == p, thr_ref[p], limit)
    column = lax.broadcasted_iota(jnp.int32, (parents, feat_dev), 1) + my_feat * feat_dev
    select = jnp.where(column == split, 1.0, 0.0).astype(BF16)
    loads[0].wait()
    codes = codes_vm[...].astype(F32).astype(BF16)
    picked = lax.dot_general(select, codes, NT, preferred_element_type=F32)
    node = node_vm[...].astype(F32)
    index = lax.broadcasted_iota(jnp.int32, (parents, rows), 0).astype(F32)
    over = (picked > limit[:, :1].astype(F32)) & (node == index)
    flags[0] = jnp.sum(jnp.where(over, 1.0, 0.0), axis=0, keepdims=True)

    eye = (
        lax.broadcasted_iota(jnp.int32, (feat_dev, feat_dev), 0)
        == lax.broadcasted_iota(jnp.int32, (feat_dev, feat_dev), 1)
    )
    eye = jnp.where(eye, 1.0, 0.0).astype(BF16)
    across = lax.dot_general(eye, codes, NT, preferred_element_type=F32)
    codes_t[...] = across.astype(BF16).reshape(nr, feats, rows)

    pl.semaphore_wait(barrier, nf + nr - 2)
    flag_copies = []
    for t in range(1, nf):
        copy = pltpu.make_async_remote_copy(
            src_ref=flags.at[0], dst_ref=flags.at[nf - t],
            send_sem=flag_send.at[t - 1], recv_sem=flag_recv.at[t - 1],
            device_id={"feat": lax.rem(my_feat + t, nf)}, device_id_type=MESH,
        )
        copy.start()
        flag_copies.append(copy)

    code_copies = []
    for t in range(1, nr):
        dest = lax.rem(my_row + t, nr)
        copy = pltpu.make_async_remote_copy(
            src_ref=codes_t.at[dest], dst_ref=codes_in.at[nr - t - 1],
            send_sem=code_send.at[t - 1], recv_sem=code_recv.at[t - 1],
            device_id={"row": dest}, device_id_type=MESH,
        )
        copy.start()
        code_copies.append(copy)
    codes32[...] = codes_t[my_row].astype(F32)

    for copy in flag_copies:
        copy.wait()
    right = jnp.sum(flags[...], axis=0)
    meta[0, 0:1, :] = 2.0 * node + right
    meta[0, 1:2, :] = as_row(grad_vm[...].astype(F32))
    meta[0, 2:3, :] = as_row(hess_vm[...].astype(F32))
    meta[0, 3:4, :] = jnp.zeros((1, rows), F32)
    meta_copies = []
    for t in range(1, nr):
        copy = pltpu.make_async_remote_copy(
            src_ref=meta.at[0], dst_ref=meta.at[nr - t],
            send_sem=meta_send.at[t - 1], recv_sem=meta_recv.at[t - 1],
            device_id={"row": lax.rem(my_row + t, nr)}, device_id_type=MESH,
        )
        copy.start()
        meta_copies.append(copy)

    weigh(w, meta, 0, 0)

    def first(i, carry):
        for j in range(group):
            feature = i * group + j
            acc[feature] = left_sums(w, codes32, feature, 0, rows)
        return carry

    lax.fori_loop(0, feats // group, first, 0)

    for t in range(1, nr):
        code_copies[t - 1].wait()
        meta_copies[t - 1].wait()
    for slot in range(1, nr):
        at = (slot - 1) * rows
        codes_out[:, at : at + rows] = codes_in[slot - 1].astype(F32)
        weigh(w_out, meta, slot, at)


def gain_kernel(rows, acc, codes32, w, out_hbm, out_vm, more_sums, out_sem):
    feats, others = codes32.shape[0], codes32.shape[1] // rows
    nodes = w.shape[0] // 2
    group = largest_divisor(feats, GROUP)
    span = largest_divisor(others, 3)
    width = span * rows
    middle = others // span - 1

    def more(step, carry):
        start = pl.multiple_of(step * width, rows)

        def some(i, inner):
            for j in range(group):
                feature = i * group + j
                part = left_sums(w, codes32, feature, start, width)
                more_sums[feature] += part
            return inner

        return lax.fori_loop(0, feats // group, some, carry)

    if middle:
        more_sums[...] = jnp.zeros(more_sums.shape, F32)
        lax.fori_loop(0, middle, more, 0)

    def last(i, carry):
        for j in range(group):
            feature = i * group + j
            left = acc[feature] + left_sums(w, codes32, feature, middle * width, width)
            if middle:
                left = left + more_sums[feature]
            grad_left, hess_left = left[:nodes], left[nodes:]
            grad_all, hess_all = grad_left[:, BINS - 1 :], hess_left[:, BINS - 1 :]
            grad_right, hess_right = grad_all - grad_left, hess_all - hess_left
            value = grad_left * grad_left / (hess_left + 1.0)
            value += grad_right * grad_right / (hess_right + 1.0)
            out_vm[feature] = 0.5 * (value - grad_all * grad_all / (hess_all + 1.0))
        at = pl.ds(i * group, group)
        pltpu.make_async_copy(out_vm.at[at], out_hbm.at[at], out_sem).start()
        return carry

    lax.fori_loop(0, feats // group, last, 0)
    pltpu.make_async_copy(out_vm, out_hbm, out_sem).wait()


def local(nr, nf, codes, node_ids, grads, hessians, split_feature, threshold):
    rows, feat_dev = codes.shape
    feats = feat_dev // nr
    parents = split_feature.shape[0]
    nodes = 2 * parents
    others = (nr - 1) * rows
    middle = (nr - 1) // largest_divisor(nr - 1, 3) - 1
    vmem, smem = pltpu.VMEM, pltpu.SMEM
    dma = pltpu.SemaphoreType.DMA
    in_vmem, in_hbm = pl.BlockSpec(memory_space=vmem), pl.BlockSpec(memory_space=pltpu.HBM)
    block = (rows // 128, 128)
    acc, codes32, w = pl.pallas_call(
        functools.partial(gather_kernel, nr, nf),
        out_shape=(
            jax.ShapeDtypeStruct((feats, 2 * nodes, BINS), F32),
            jax.ShapeDtypeStruct((feats, others), F32),
            jax.ShapeDtypeStruct((2 * nodes, others), BF16),
        ),
        in_specs=[in_hbm] * 6,
        out_specs=(in_vmem, in_vmem, in_vmem),
        scratch_shapes=[
            smem((parents,), jnp.int32),
            smem((parents,), jnp.int32),
            vmem((rows, feat_dev), jnp.int32),
            vmem((1, rows), jnp.int32),
            vmem(block, BF16),
            vmem(block, BF16),
            vmem((nr, feats, rows), BF16),
            vmem((nr - 1, feats, rows), BF16),
            vmem((feats, rows), F32),
            vmem((nf, 1, rows), F32),
            vmem((nr, 4, rows), F32),
            vmem((2 * nodes, rows), BF16),
            dma((6,)),
            dma((nf - 1,)),
            dma((nf - 1,)),
            dma((nr - 1,)),
            dma((nr - 1,)),
            dma((nr - 1,)),
            dma((nr - 1,)),
        ],
        compiler_params=pltpu.CompilerParams(
            collective_id=0, has_side_effects=True, vmem_limit_bytes=32 << 20
        ),
    )(
        *(
            pltpu.with_memory_space_constraint(x, pltpu.HBM)
            for x in (
                split_feature, threshold, codes, node_ids.reshape(1, rows),
                grads.reshape(block), hessians.reshape(block),
            )
        )
    )
    return pl.pallas_call(
        functools.partial(gain_kernel, rows),
        out_shape=jax.ShapeDtypeStruct((feats, nodes, BINS), F32),
        in_specs=[in_vmem] * 3,
        out_specs=in_hbm,
        scratch_shapes=[
            vmem((feats, nodes, BINS), F32),
            vmem((feats if middle else 1, 2 * nodes, BINS), F32),
            dma,
        ],
        compiler_params=pltpu.CompilerParams(vmem_limit_bytes=32 << 20),
    )(acc, codes32, w)


def solution(mesh):
    return jax.shard_map(
        functools.partial(local, mesh.shape["row"], mesh.shape["feat"]),
        mesh=mesh,
        in_specs=(P("row", "feat"), P("row"), P("row"), P("row"), P(), P()),
        out_specs=P(("feat", "row"), None, None),
        check_vma=False,
    )
```

```python
import functools

import jax
import jax.numpy as jnp
from jax import lax
from jax.experimental import pallas as pl
from jax.experimental.pallas import tpu as pltpu
from jax.sharding import PartitionSpec as P

BINS = 256
GROUP = 16
MESH = pl.DeviceIdType.MESH
NT = (((1,), (1,)), ((), ()))
F32, BF16, FLAG = jnp.float32, jnp.bfloat16, jnp.float8_e4m3fn


def largest_divisor(number, limit):
    return max(d for d in range(1, limit + 1) if number % d == 0)


def as_row(block):
    return jnp.concatenate([block[i : i + 1] for i in range(block.shape[0])], axis=1)


def weigh(w, child, grad, hess, start):
    nodes, width = w.shape[0] // 2, child.shape[1]
    number = lax.broadcasted_iota(jnp.int32, (nodes, width), 0).astype(F32)
    member = child == number
    w[0:nodes, start : start + width] = jnp.where(member, grad, 0.0).astype(BF16)
    w[nodes:, start : start + width] = jnp.where(member, hess, 0.0).astype(BF16)


def weigh_parents(w, node, grad, hess, width):
    nodes = w.shape[0] // 2
    member = node[:, :width] == parent_number(nodes, width)
    w[0:nodes, 0:width] = jnp.where(member, grad[:, :width], 0.0).astype(BF16)
    w[nodes:, 0:width] = jnp.where(member, hess[:, :width], 0.0).astype(BF16)


def parent_number(nodes, width):
    return (lax.broadcasted_iota(jnp.int32, (nodes, width), 0) // 2).astype(F32)


def early_rows(rows):
    return rows // 2


def keep_smaller(w, lines, other, codes_post, codes_own, below_diagonal, node, right):
    nodes, early = w.shape[0] // 2, below_diagonal.shape[0]
    half = early // 2
    bit = right[:, :early]
    member = node[:, :early] == parent_number(nodes, early)
    in_all = jnp.sum(jnp.where(member, 1.0, 0.0), axis=1, keepdims=True)
    in_right = jnp.sum(jnp.where(member, bit, 0.0), axis=1, keepdims=True)
    side = jnp.where(2.0 * in_right <= in_all, 1.0, 0.0)
    odd = lax.broadcasted_iota(jnp.int32, (nodes, 1), 0) % 2
    larger = jnp.where(odd.astype(F32) == side, 0.0, 1.0)
    other[0:nodes] = jnp.broadcast_to(larger, (nodes, other.shape[1]))
    other[nodes:] = jnp.broadcast_to(larger, (nodes, other.shape[1]))
    side_row = 0.5 * jnp.sum(jnp.where(member, side, 0.0), axis=0, keepdims=True)
    chosen = bit == side_row
    ones = jnp.broadcast_to(jnp.where(chosen, 1.0, 0.0), (16, early)).astype(BF16)
    rank = jnp.dot(ones, below_diagonal[...], preferred_element_type=F32)[0:1]
    rank = jnp.where(chosen, rank, -1.0)
    place = lax.broadcasted_iota(jnp.int32, (half, early), 0).astype(F32)
    move = jnp.where(rank == place, 1.0, 0.0).astype(BF16).astype(FLAG)
    lines = lax.dot_general(
        lines[:, :early].astype(BF16), move, NT, preferred_element_type=F32
    )
    codes_post[:, 0:half] = lax.dot_general(
        codes_own[:, 0:early], move, NT, preferred_element_type=F32
    )
    number = lax.broadcasted_iota(jnp.int32, (nodes, half), 0).astype(F32)
    plus, minus = lines[0:1] == number, lines[3:4] == number
    for k in range(2):
        value = lines[k + 1 : k + 2]
        value = jnp.where(plus, value, jnp.where(minus, -value, 0.0))
        w[k * nodes : (k + 1) * nodes, 0:half] = value.astype(BF16)


def below(codes32, feature, start, width):
    code = codes32[pl.ds(feature, 1), pl.ds(start, width)].astype(BF16)
    bins = lax.broadcasted_iota(jnp.int32, (BINS, width), 0).astype(F32).astype(BF16)
    one, zero = jnp.ones((), FLAG), jnp.zeros((), FLAG)
    return jnp.where(bins >= code, one, zero)


def left_sums(w, codes32, feature, start, width):
    return lax.dot_general(
        w[:, pl.ds(start, width)], below(codes32, feature, start, width), NT,
        preferred_element_type=F32,
    )


def gather_kernel(
    nr, nf, sf_hbm, thr_hbm, codes_hbm, node_hbm, grad_hbm, hess_hbm,
    acc, codes_out, w_out,
    sf_ref, thr_ref, codes_vm, node_vm, grad_vm, hess_vm,
    codes_t, codes_in, codes32, codes_post, flags, child, weight, w, other, below_diagonal,
    load_sem, flag_send, flag_recv, code_send, code_recv, child_send, child_recv,
    weight_send, weight_recv,
):
    rows, feat_dev = codes_vm.shape
    feats = feat_dev // nr
    parents = sf_ref.shape[0]
    nodes = 2 * parents
    my_row, my_feat = lax.axis_index("row"), lax.axis_index("feat")
    group = largest_divisor(feats, GROUP)

    loads = []
    for i, (source, target) in enumerate(
        (
            (codes_hbm, codes_vm), (sf_hbm, sf_ref), (thr_hbm, thr_ref),
            (node_hbm, node_vm), (grad_hbm, grad_vm), (hess_hbm, hess_vm),
        )
    ):
        load = pltpu.make_async_copy(source, target, load_sem.at[i])
        load.start()
        loads.append(load)
    barrier = pltpu.get_barrier_semaphore()
    for t in range(1, nf):
        pl.semaphore_signal(
            barrier, inc=1, device_id={"feat": lax.rem(my_feat + t, nf)}, device_id_type=MESH
        )
    for t in range(1, nr):
        pl.semaphore_signal(
            barrier, inc=1, device_id={"row": lax.rem(my_row + t, nr)}, device_id_type=MESH
        )

    for load in loads[1:]:
        load.wait()
    parent = lax.broadcasted_iota(jnp.int32, (parents, feat_dev), 0)
    split = jnp.zeros((parents, feat_dev), jnp.int32)
    limit = jnp.zeros((parents, 128), jnp.int32)
    for p in range(parents):
        split = jnp.where(parent == p, sf_ref[p], split)
        limit = jnp.where(parent[:, :128] == p, thr_ref[p], limit)
    column = lax.broadcasted_iota(jnp.int32, (parents, feat_dev), 1) + my_feat * feat_dev
    select = jnp.where(column == split, 1.0, 0.0).astype(BF16)
    loads[0].wait()
    codes = codes_vm[...].astype(F32).astype(BF16)
    picked = lax.dot_general(select, codes, NT, preferred_element_type=F32)
    node = node_vm[...].astype(F32)
    index = lax.broadcasted_iota(jnp.int32, (parents, rows), 0).astype(F32)
    over = (picked > limit[:, :1].astype(F32)) & (node == index)
    flags[0] = jnp.sum(jnp.where(over, 1.0, 0.0), axis=0, keepdims=True)

    eye = (
        lax.broadcasted_iota(jnp.int32, (feat_dev, feat_dev), 0)
        == lax.broadcasted_iota(jnp.int32, (feat_dev, feat_dev), 1)
    )
    eye = jnp.where(eye, 1.0, 0.0).astype(BF16)
    across = lax.dot_general(eye, codes, NT, preferred_element_type=F32)
    codes_t[...] = across.astype(BF16).reshape(nr, feats, rows)

    grad, hess = as_row(grad_vm[...].astype(F32)), as_row(hess_vm[...].astype(F32))
    weight[0, 0:1, :] = grad
    weight[0, 1:2, :] = hess
    early = early_rows(rows)
    half = early // 2
    below_diagonal[...] = jnp.where(
        lax.broadcasted_iota(jnp.int32, (early, early), 0)
        < lax.broadcasted_iota(jnp.int32, (early, early), 1),
        1.0, 0.0,
    ).astype(BF16).astype(FLAG)

    pl.semaphore_wait(barrier, nf + nr - 2)
    flag_copies = []
    for t in range(1, nf):
        copy = pltpu.make_async_remote_copy(
            src_ref=flags.at[0], dst_ref=flags.at[nf - t],
            send_sem=flag_send.at[t - 1], recv_sem=flag_recv.at[t - 1],
            device_id={"feat": lax.rem(my_feat + t, nf)}, device_id_type=MESH,
        )
        copy.start()
        flag_copies.append(copy)

    def to_rows(ref, send, recv):
        copies = []
        for t in range(1, nr):
            copy = pltpu.make_async_remote_copy(
                src_ref=ref.at[0], dst_ref=ref.at[nr - t],
                send_sem=send.at[t - 1], recv_sem=recv.at[t - 1],
                device_id={"row": lax.rem(my_row + t, nr)}, device_id_type=MESH,
            )
            copy.start()
            copies.append(copy)
        return copies

    weight_copies = to_rows(weight, weight_send, weight_recv)
    code_copies = []

    def send_codes(part):
        size = feats // 2
        for t in range(1, nr):
            dest = lax.rem(my_row + t, nr)
            at = pl.ds(part * size, size)
            copy = pltpu.make_async_remote_copy(
                src_ref=codes_t.at[dest, at], dst_ref=codes_in.at[nr - t - 1, at],
                send_sem=code_send.at[part, t - 1], recv_sem=code_recv.at[part, t - 1],
                device_id={"row": dest}, device_id_type=MESH,
            )
            copy.start()
            code_copies.append(copy)

    send_codes(0)
    codes32[...] = codes_t[my_row].astype(F32)
    after = half + rows - early
    weigh_parents(w, node, grad, hess, early)

    def parents_first(i, carry):
        for j in range(group):
            feature = i * group + j
            acc[feature] = left_sums(w, codes32, feature, 0, early)
        return carry

    lax.fori_loop(0, feats // group, parents_first, 0)
    for copy in flag_copies:
        copy.wait()
    right = jnp.sum(flags[...], axis=0)
    mine = 2.0 * node + right
    child[0] = mine
    child_copies = to_rows(child, child_send, child_recv)
    send_codes(1)

    lines = jnp.concatenate([mine, grad, hess, 2.0 * node + 1.0 - right], axis=0)
    keep_smaller(w, lines, other, codes_post, codes_t.at[my_row], below_diagonal, node, right)
    weigh(w, mine[:, early:], grad[:, early:], hess[:, early:], half)
    codes_post[:, half:] = codes32[:, early:]

    def own_rest(i, carry):
        for j in range(group):
            feature = i * group + j
            part = left_sums(w, codes_post, feature, 0, after)
            acc[feature] = acc[feature] * other[...] + part
        return carry

    lax.fori_loop(0, feats // group, own_rest, 0)

    for t in range(1, nr):
        weight_copies[t - 1].wait()
        child_copies[t - 1].wait()
    for copy in code_copies:
        copy.wait()
    for slot in range(1, nr):
        at = (slot - 1) * rows
        codes_out[:, at : at + rows] = codes_in[slot - 1].astype(F32)
        weigh(w_out, child[slot], weight[slot, 0:1, :], weight[slot, 1:2, :], at)


def gain_kernel(rows, acc, codes32, w, out_hbm, out_vm, more_sums, out_sem):
    feats, others = codes32.shape[0], codes32.shape[1] // rows
    nodes = w.shape[0] // 2
    group = largest_divisor(feats, 2 * GROUP)
    step_out = largest_divisor(group, 2)
    span = largest_divisor(others, 3)
    width = span * rows
    middle = others // span - 1

    def more(step, carry):
        start = pl.multiple_of(step * width, rows)

        def some(i, inner):
            for j in range(group):
                feature = i * group + j
                part = left_sums(w, codes32, feature, start, width)
                more_sums[feature] += part
            return inner

        return lax.fori_loop(0, feats // group, some, carry)

    if middle:
        more_sums[...] = jnp.zeros(more_sums.shape, F32)
        lax.fori_loop(0, middle, more, 0)

    def last(i, carry):
        for j in range(group):
            feature = i * group + j
            left = acc[feature] + left_sums(w, codes32, feature, middle * width, width)
            if middle:
                left = left + more_sums[feature]
            grad_left, hess_left = left[:nodes], left[nodes:]
            grad_all, hess_all = grad_left[:, BINS - 1 :], hess_left[:, BINS - 1 :]
            grad_right, hess_right = grad_all - grad_left, hess_all - hess_left
            value = grad_left * grad_left / (hess_left + 1.0)
            value += grad_right * grad_right / (hess_right + 1.0)
            out_vm[feature] = 0.5 * (value - grad_all * grad_all / (hess_all + 1.0))
            if (j + 1) % step_out == 0:
                at = pl.ds(feature + 1 - step_out, step_out)
                pltpu.make_async_copy(out_vm.at[at], out_hbm.at[at], out_sem).start()
        return carry

    lax.fori_loop(0, feats // group, last, 0)
    pltpu.make_async_copy(out_vm, out_hbm, out_sem).wait()


def local(nr, nf, codes, node_ids, grads, hessians, split_feature, threshold):
    rows, feat_dev = codes.shape
    feats = feat_dev // nr
    parents = split_feature.shape[0]
    nodes = 2 * parents
    others = (nr - 1) * rows
    middle = (nr - 1) // largest_divisor(nr - 1, 3) - 1
    early = early_rows(rows)
    vmem, smem = pltpu.VMEM, pltpu.SMEM
    dma = pltpu.SemaphoreType.DMA
    in_vmem, in_hbm = pl.BlockSpec(memory_space=vmem), pl.BlockSpec(memory_space=pltpu.HBM)
    block = (rows // 128, 128)
    acc, codes32, w = pl.pallas_call(
        functools.partial(gather_kernel, nr, nf),
        out_shape=(
            jax.ShapeDtypeStruct((feats, 2 * nodes, BINS), F32),
            jax.ShapeDtypeStruct((feats, others), F32),
            jax.ShapeDtypeStruct((2 * nodes, others), BF16),
        ),
        in_specs=[in_hbm] * 6,
        out_specs=(in_vmem, in_vmem, in_vmem),
        scratch_shapes=[
            smem((parents,), jnp.int32),
            smem((parents,), jnp.int32),
            vmem((rows, feat_dev), jnp.int32),
            vmem((1, rows), jnp.int32),
            vmem(block, BF16),
            vmem(block, BF16),
            vmem((nr, feats, rows), BF16),
            vmem((nr - 1, feats, rows), BF16),
            vmem((feats, rows), F32),
            vmem((feats, rows - early + early // 2), F32),
            vmem((nf, 1, rows), F32),
            vmem((nr, 1, rows), F32),
            vmem((nr, 2, rows), F32),
            vmem((2 * nodes, rows), BF16),
            vmem((2 * nodes, BINS), F32),
            vmem((early, early), FLAG),
            dma((6,)),
            dma((nf - 1,)),
            dma((nf - 1,)),
            dma((2, nr - 1)),
            dma((2, nr - 1)),
            dma((nr - 1,)),
            dma((nr - 1,)),
            dma((nr - 1,)),
            dma((nr - 1,)),
        ],
        compiler_params=pltpu.CompilerParams(
            collective_id=0, has_side_effects=True, vmem_limit_bytes=32 << 20
        ),
    )(
        *(
            pltpu.with_memory_space_constraint(x, pltpu.HBM)
            for x in (
                split_feature, threshold, codes, node_ids.reshape(1, rows),
                grads.reshape(block), hessians.reshape(block),
            )
        )
    )
    return pl.pallas_call(
        functools.partial(gain_kernel, rows),
        out_shape=jax.ShapeDtypeStruct((feats, nodes, BINS), F32),
        in_specs=[in_vmem] * 3,
        out_specs=in_hbm,
        scratch_shapes=[
            vmem((feats, nodes, BINS), F32),
            vmem((feats if middle else 1, 2 * nodes, BINS), F32),
            dma,
        ],
        compiler_params=pltpu.CompilerParams(vmem_limit_bytes=32 << 20),
    )(acc, codes32, w)


def solution(mesh):
    return jax.shard_map(
        functools.partial(local, mesh.shape["row"], mesh.shape["feat"]),
        mesh=mesh,
        in_specs=(P("row", "feat"), P("row"), P("row"), P("row"), P(), P()),
        out_specs=P(("feat", "row"), None, None),
        check_vma=False,
    )
```

```python
import functools

import jax
import jax.numpy as jnp
from jax import lax
from jax.experimental import pallas as pl
from jax.experimental.pallas import tpu as pltpu
from jax.sharding import PartitionSpec as P

BINS = 256
GROUP = 16
MESH = pl.DeviceIdType.MESH
NT = (((1,), (1,)), ((), ()))
F32, BF16, FLAG = jnp.float32, jnp.bfloat16, jnp.float8_e4m3fn


def largest_divisor(number, limit):
    return max(d for d in range(1, limit + 1) if number % d == 0)


def as_row(block):
    return jnp.concatenate([block[i : i + 1] for i in range(block.shape[0])], axis=1)


def weigh(w, child, grad, hess, start):
    nodes, width = w.shape[0] // 2, child.shape[1]
    number = lax.broadcasted_iota(jnp.int32, (nodes, width), 0).astype(F32)
    member = child == number
    w[0:nodes, start : start + width] = jnp.where(member, grad, 0.0).astype(BF16)
    w[nodes:, start : start + width] = jnp.where(member, hess, 0.0).astype(BF16)


def weigh_parents(w, node, grad, hess, width):
    nodes = w.shape[0] // 2
    member = node[:, :width] == parent_number(nodes, width)
    w[0:nodes, 0:width] = jnp.where(member, grad[:, :width], 0.0).astype(BF16)
    w[nodes:, 0:width] = jnp.where(member, hess[:, :width], 0.0).astype(BF16)


def parent_number(nodes, width):
    return (lax.broadcasted_iota(jnp.int32, (nodes, width), 0) // 2).astype(F32)


def early_rows(rows):
    return rows // 2


def keep_smaller(w, lines, other, codes_post, codes_own, below_diagonal, node, right):
    nodes, early = w.shape[0] // 2, below_diagonal.shape[0]
    half = early // 2
    bit = right[:, :early]
    member = node[:, :early] == parent_number(nodes, early)
    in_all = jnp.sum(jnp.where(member, 1.0, 0.0), axis=1, keepdims=True)
    in_right = jnp.sum(jnp.where(member, bit, 0.0), axis=1, keepdims=True)
    side = jnp.where(2.0 * in_right <= in_all, 1.0, 0.0)
    odd = lax.broadcasted_iota(jnp.int32, (nodes, 1), 0) % 2
    larger = jnp.where(odd.astype(F32) == side, 0.0, 1.0)
    other[0:nodes] = jnp.broadcast_to(larger, (nodes, other.shape[1]))
    other[nodes:] = jnp.broadcast_to(larger, (nodes, other.shape[1]))
    side_row = 0.5 * jnp.sum(jnp.where(member, side, 0.0), axis=0, keepdims=True)
    chosen = bit == side_row
    ones = jnp.broadcast_to(jnp.where(chosen, 1.0, 0.0), (16, early)).astype(BF16)
    rank = jnp.dot(ones, below_diagonal[...], preferred_element_type=F32)[0:1]
    rank = jnp.where(chosen, rank, -1.0)
    place = lax.broadcasted_iota(jnp.int32, (half, early), 0).astype(F32)
    move = jnp.where(rank == place, 1.0, 0.0).astype(BF16).astype(FLAG)
    lines = lax.dot_general(
        lines[:, :early].astype(BF16), move, NT, preferred_element_type=F32
    )
    codes_post[:, 0:half] = lax.dot_general(
        codes_own[:, 0:early], move, NT, preferred_element_type=F32
    )
    number = lax.broadcasted_iota(jnp.int32, (nodes, half), 0).astype(F32)
    plus, minus = lines[0:1] == number, lines[3:4] == number
    for k in range(2):
        value = lines[k + 1 : k + 2]
        value = jnp.where(plus, value, jnp.where(minus, -value, 0.0))
        w[k * nodes : (k + 1) * nodes, 0:half] = value.astype(BF16)


def below(codes32, feature, start, width):
    code = codes32[pl.ds(feature, 1), pl.ds(start, width)].astype(BF16)
    bins = lax.broadcasted_iota(jnp.int32, (BINS, width), 0).astype(F32).astype(BF16)
    one, zero = jnp.ones((), FLAG), jnp.zeros((), FLAG)
    return jnp.where(bins >= code, one, zero)


def left_sums(w, codes32, feature, start, width):
    return lax.dot_general(
        w[:, pl.ds(start, width)], below(codes32, feature, start, width), NT,
        preferred_element_type=F32,
    )


def gather_kernel(
    nr, nf, sf_hbm, thr_hbm, codes_hbm, node_hbm, grad_hbm, hess_hbm,
    acc, codes_out, w_out,
    sf_ref, thr_ref, codes_vm, node_vm, grad_vm, hess_vm,
    codes_t, codes_in, codes32, codes_post, flags, child, weight, w, other, below_diagonal,
    load_sem, flag_send, flag_recv, code_send, code_recv, child_send, child_recv,
    weight_send, weight_recv,
):
    rows, feat_dev = codes_vm.shape
    feats = feat_dev // nr
    parents = sf_ref.shape[0]
    nodes = 2 * parents
    my_row, my_feat = lax.axis_index("row"), lax.axis_index("feat")
    group = largest_divisor(feats, 2 * GROUP)

    loads = []
    for i, (source, target) in enumerate(
        (
            (codes_hbm, codes_vm), (sf_hbm, sf_ref), (thr_hbm, thr_ref),
            (node_hbm, node_vm), (grad_hbm, grad_vm), (hess_hbm, hess_vm),
        )
    ):
        load = pltpu.make_async_copy(source, target, load_sem.at[i])
        load.start()
        loads.append(load)
    barrier = pltpu.get_barrier_semaphore()
    for t in range(1, nf):
        pl.semaphore_signal(
            barrier, inc=1, device_id={"feat": lax.rem(my_feat + t, nf)}, device_id_type=MESH
        )
    for t in range(1, nr):
        pl.semaphore_signal(
            barrier, inc=1, device_id={"row": lax.rem(my_row + t, nr)}, device_id_type=MESH
        )

    for load in loads[1:]:
        load.wait()
    parent = lax.broadcasted_iota(jnp.int32, (parents, feat_dev), 0)
    split = jnp.zeros((parents, feat_dev), jnp.int32)
    limit = jnp.zeros((parents, 128), jnp.int32)
    for p in range(parents):
        split = jnp.where(parent == p, sf_ref[p], split)
        limit = jnp.where(parent[:, :128] == p, thr_ref[p], limit)
    column = lax.broadcasted_iota(jnp.int32, (parents, feat_dev), 1) + my_feat * feat_dev
    select = jnp.where(column == split, 1.0, 0.0).astype(BF16)
    loads[0].wait()
    codes = codes_vm[...].astype(F32).astype(BF16)
    picked = lax.dot_general(select, codes, NT, preferred_element_type=F32)
    node = node_vm[...].astype(F32)
    index = lax.broadcasted_iota(jnp.int32, (parents, rows), 0).astype(F32)
    over = (picked > limit[:, :1].astype(F32)) & (node == index)
    flags[0] = jnp.sum(jnp.where(over, 1.0, 0.0), axis=0, keepdims=True)

    eye = (
        lax.broadcasted_iota(jnp.int32, (feat_dev, feat_dev), 0)
        == lax.broadcasted_iota(jnp.int32, (feat_dev, feat_dev), 1)
    )
    eye = jnp.where(eye, 1.0, 0.0).astype(BF16)
    across = lax.dot_general(eye, codes, NT, preferred_element_type=F32)
    codes_t[...] = across.astype(BF16).reshape(nr, feats, rows)

    grad, hess = as_row(grad_vm[...].astype(F32)), as_row(hess_vm[...].astype(F32))
    weight[0, 0:1, :] = grad
    weight[0, 1:2, :] = hess
    early = early_rows(rows)
    half = early // 2
    below_diagonal[...] = jnp.where(
        lax.broadcasted_iota(jnp.int32, (early, early), 0)
        < lax.broadcasted_iota(jnp.int32, (early, early), 1),
        1.0, 0.0,
    ).astype(BF16).astype(FLAG)

    pl.semaphore_wait(barrier, nf + nr - 2)
    flag_copies = []
    for t in range(1, nf):
        copy = pltpu.make_async_remote_copy(
            src_ref=flags.at[0], dst_ref=flags.at[nf - t],
            send_sem=flag_send.at[t - 1], recv_sem=flag_recv.at[t - 1],
            device_id={"feat": lax.rem(my_feat + t, nf)}, device_id_type=MESH,
        )
        copy.start()
        flag_copies.append(copy)

    def to_rows(ref, send, recv):
        copies = []
        for t in range(1, nr):
            copy = pltpu.make_async_remote_copy(
                src_ref=ref.at[0], dst_ref=ref.at[nr - t],
                send_sem=send.at[t - 1], recv_sem=recv.at[t - 1],
                device_id={"row": lax.rem(my_row + t, nr)}, device_id_type=MESH,
            )
            copy.start()
            copies.append(copy)
        return copies

    weight_copies = to_rows(weight, weight_send, weight_recv)
    code_copies = []

    def send_codes(part):
        size = feats // 2
        for t in range(1, nr):
            dest = lax.rem(my_row + t, nr)
            at = pl.ds(part * size, size)
            copy = pltpu.make_async_remote_copy(
                src_ref=codes_t.at[dest, at], dst_ref=codes_in.at[nr - t - 1, at],
                send_sem=code_send.at[part, t - 1], recv_sem=code_recv.at[part, t - 1],
                device_id={"row": dest}, device_id_type=MESH,
            )
            copy.start()
            code_copies.append(copy)

    send_codes(0)
    codes32[...] = codes_t[my_row].astype(F32)
    after = half + rows - early
    weigh_parents(w, node, grad, hess, early)

    def parents_first(i, carry):
        for j in range(group):
            feature = i * group + j
            acc[feature] = left_sums(w, codes32, feature, 0, early)
        return carry

    lax.fori_loop(0, feats // group, parents_first, 0)
    for copy in flag_copies:
        copy.wait()
    right = jnp.sum(flags[...], axis=0)
    mine = 2.0 * node + right
    child[0] = mine
    child_copies = to_rows(child, child_send, child_recv)
    send_codes(1)

    lines = jnp.concatenate([mine, grad, hess, 2.0 * node + 1.0 - right], axis=0)
    keep_smaller(w, lines, other, codes_post, codes_t.at[my_row], below_diagonal, node, right)
    weigh(w, mine[:, early:], grad[:, early:], hess[:, early:], half)
    codes_post[:, half:] = codes32[:, early:]

    def own_rest(i, carry):
        for j in range(group):
            feature = i * group + j
            part = left_sums(w, codes_post, feature, 0, after)
            acc[feature] = acc[feature] * other[...] + part
        return carry

    lax.fori_loop(0, feats // group, own_rest, 0)

    for t in range(1, nr):
        weight_copies[t - 1].wait()
        child_copies[t - 1].wait()
    for copy in code_copies:
        copy.wait()
    for slot in range(1, nr):
        at = (slot - 1) * rows
        codes_out[:, at : at + rows] = codes_in[slot - 1].astype(F32)
        weigh(w_out, child[slot], weight[slot, 0:1, :], weight[slot, 1:2, :], at)


def gain_kernel(rows, acc, codes32, w, out_hbm, out_vm, more_sums, out_sem):
    feats, others = codes32.shape[0], codes32.shape[1] // rows
    nodes = w.shape[0] // 2
    group = largest_divisor(feats, 4 * GROUP)
    step_out = largest_divisor(group, 2)
    span = largest_divisor(others, 3)
    width = span * rows
    middle = others // span - 1

    def more(step, carry):
        start = pl.multiple_of(step * width, rows)

        def some(i, inner):
            for j in range(group):
                feature = i * group + j
                part = left_sums(w, codes32, feature, start, width)
                more_sums[feature] += part
            return inner

        return lax.fori_loop(0, feats // group, some, carry)

    if middle:
        more_sums[...] = jnp.zeros(more_sums.shape, F32)
        lax.fori_loop(0, middle, more, 0)

    def last(i, carry):
        for j in range(group):
            feature = i * group + j
            left = acc[feature] + left_sums(w, codes32, feature, middle * width, width)
            if middle:
                left = left + more_sums[feature]
            grad_left, hess_left = left[:nodes], left[nodes:]
            grad_all, hess_all = grad_left[:, BINS - 1 :], hess_left[:, BINS - 1 :]
            grad_right, hess_right = grad_all - grad_left, hess_all - hess_left
            value = grad_left * grad_left / (hess_left + 1.0)
            value += grad_right * grad_right / (hess_right + 1.0)
            out_vm[feature] = 0.5 * (value - grad_all * grad_all / (hess_all + 1.0))
            if (j + 1) % step_out == 0:
                at = pl.ds(feature + 1 - step_out, step_out)
                pltpu.make_async_copy(out_vm.at[at], out_hbm.at[at], out_sem).start()
        return carry

    lax.fori_loop(0, feats // group, last, 0)
    pltpu.make_async_copy(out_vm, out_hbm, out_sem).wait()


def local(nr, nf, codes, node_ids, grads, hessians, split_feature, threshold):
    rows, feat_dev = codes.shape
    feats = feat_dev // nr
    parents = split_feature.shape[0]
    nodes = 2 * parents
    others = (nr - 1) * rows
    middle = (nr - 1) // largest_divisor(nr - 1, 3) - 1
    early = early_rows(rows)
    vmem, smem = pltpu.VMEM, pltpu.SMEM
    dma = pltpu.SemaphoreType.DMA
    in_vmem, in_hbm = pl.BlockSpec(memory_space=vmem), pl.BlockSpec(memory_space=pltpu.HBM)
    block = (rows // 128, 128)
    acc, codes32, w = pl.pallas_call(
        functools.partial(gather_kernel, nr, nf),
        out_shape=(
            jax.ShapeDtypeStruct((feats, 2 * nodes, BINS), F32),
            jax.ShapeDtypeStruct((feats, others), F32),
            jax.ShapeDtypeStruct((2 * nodes, others), BF16),
        ),
        in_specs=[in_hbm] * 6,
        out_specs=(in_vmem, in_vmem, in_vmem),
        scratch_shapes=[
            smem((parents,), jnp.int32),
            smem((parents,), jnp.int32),
            vmem((rows, feat_dev), jnp.int32),
            vmem((1, rows), jnp.int32),
            vmem(block, BF16),
            vmem(block, BF16),
            vmem((nr, feats, rows), BF16),
            vmem((nr - 1, feats, rows), BF16),
            vmem((feats, rows), F32),
            vmem((feats, rows - early + early // 2), F32),
            vmem((nf, 1, rows), F32),
            vmem((nr, 1, rows), F32),
            vmem((nr, 2, rows), F32),
            vmem((2 * nodes, rows), BF16),
            vmem((2 * nodes, BINS), F32),
            vmem((early, early), FLAG),
            dma((6,)),
            dma((nf - 1,)),
            dma((nf - 1,)),
            dma((2, nr - 1)),
            dma((2, nr - 1)),
            dma((nr - 1,)),
            dma((nr - 1,)),
            dma((nr - 1,)),
            dma((nr - 1,)),
        ],
        compiler_params=pltpu.CompilerParams(
            collective_id=0, has_side_effects=True, vmem_limit_bytes=32 << 20
        ),
    )(
        *(
            pltpu.with_memory_space_constraint(x, pltpu.HBM)
            for x in (
                split_feature, threshold, codes, node_ids.reshape(1, rows),
                grads.reshape(block), hessians.reshape(block),
            )
        )
    )
    return pl.pallas_call(
        functools.partial(gain_kernel, rows),
        out_shape=jax.ShapeDtypeStruct((feats, nodes, BINS), F32),
        in_specs=[in_vmem] * 3,
        out_specs=in_hbm,
        scratch_shapes=[
            vmem((feats, nodes, BINS), F32),
            vmem((feats if middle else 1, 2 * nodes, BINS), F32),
            dma,
        ],
        compiler_params=pltpu.CompilerParams(vmem_limit_bytes=32 << 20),
    )(acc, codes32, w)


def solution(mesh):
    return jax.shard_map(
        functools.partial(local, mesh.shape["row"], mesh.shape["feat"]),
        mesh=mesh,
        in_specs=(P("row", "feat"), P("row"), P("row"), P("row"), P(), P()),
        out_specs=P(("feat", "row"), None, None),
        check_vma=False,
    )
```

```python
import functools

import jax
import jax.numpy as jnp
from jax import lax
from jax.experimental import pallas as pl
from jax.experimental.pallas import tpu as pltpu
from jax.sharding import PartitionSpec as P

BINS = 256
GROUP = 16
MESH = pl.DeviceIdType.MESH
NT = (((1,), (1,)), ((), ()))
F32, BF16, FLAG = jnp.float32, jnp.bfloat16, jnp.float8_e4m3fn


def largest_divisor(number, limit):
    return max(d for d in range(1, limit + 1) if number % d == 0)


def as_row(block):
    return jnp.concatenate([block[i : i + 1] for i in range(block.shape[0])], axis=1)


def weigh(w, child, grad, hess, start):
    nodes, width = w.shape[0] // 2, child.shape[1]
    number = lax.broadcasted_iota(jnp.int32, (nodes, width), 0).astype(F32)
    member = child == number
    w[0:nodes, start : start + width] = jnp.where(member, grad, 0.0).astype(BF16)
    w[nodes:, start : start + width] = jnp.where(member, hess, 0.0).astype(BF16)


def weigh_parents(w, node, grad, hess, width):
    nodes = w.shape[0] // 2
    member = node[:, :width] == parent_number(nodes, width)
    w[0:nodes, 0:width] = jnp.where(member, grad[:, :width], 0.0).astype(BF16)
    w[nodes:, 0:width] = jnp.where(member, hess[:, :width], 0.0).astype(BF16)


def parent_number(nodes, width):
    return (lax.broadcasted_iota(jnp.int32, (nodes, width), 0) // 2).astype(F32)


def early_rows(rows):
    return rows // 2


def keep_smaller(w, lines, other, codes_post, codes_own, below_diagonal, node, right):
    nodes, early = w.shape[0] // 2, below_diagonal.shape[0]
    half = early // 2
    bit = right[:, :early]
    member = node[:, :early] == parent_number(nodes, early)
    in_all = jnp.sum(jnp.where(member, 1.0, 0.0), axis=1, keepdims=True)
    in_right = jnp.sum(jnp.where(member, bit, 0.0), axis=1, keepdims=True)
    side = jnp.where(2.0 * in_right <= in_all, 1.0, 0.0)
    odd = lax.broadcasted_iota(jnp.int32, (nodes, 1), 0) % 2
    larger = jnp.where(odd.astype(F32) == side, 0.0, 1.0)
    other[0:nodes] = jnp.broadcast_to(larger, (nodes, other.shape[1]))
    other[nodes:] = jnp.broadcast_to(larger, (nodes, other.shape[1]))
    side_row = 0.5 * jnp.sum(jnp.where(member, side, 0.0), axis=0, keepdims=True)
    chosen = bit == side_row
    ones = jnp.broadcast_to(jnp.where(chosen, 1.0, 0.0), (16, early)).astype(BF16)
    rank = jnp.dot(ones, below_diagonal[...], preferred_element_type=F32)[0:1]
    rank = jnp.where(chosen, rank, -1.0)
    place = lax.broadcasted_iota(jnp.int32, (half, early), 0).astype(F32)
    move = jnp.where(rank == place, 1.0, 0.0).astype(BF16).astype(FLAG)
    lines = lax.dot_general(
        lines[:, :early].astype(BF16), move, NT, preferred_element_type=F32
    )
    codes_post[:, 0:half] = lax.dot_general(
        codes_own[:, 0:early], move, NT, preferred_element_type=F32
    )
    number = lax.broadcasted_iota(jnp.int32, (nodes, half), 0).astype(F32)
    plus, minus = lines[0:1] == number, lines[3:4] == number
    for k in range(2):
        value = lines[k + 1 : k + 2]
        value = jnp.where(plus, value, jnp.where(minus, -value, 0.0))
        w[k * nodes : (k + 1) * nodes, 0:half] = value.astype(BF16)


def below(codes32, feature, start, width):
    code = codes32[pl.ds(feature, 1), pl.ds(start, width)].astype(BF16)
    bins = lax.broadcasted_iota(jnp.int32, (BINS, width), 0).astype(F32).astype(BF16)
    one, zero = jnp.ones((), FLAG), jnp.zeros((), FLAG)
    return jnp.where(bins >= code, one, zero)


def left_sums(w, codes32, feature, start, width):
    return lax.dot_general(
        w[:, pl.ds(start, width)], below(codes32, feature, start, width), NT,
        preferred_element_type=F32,
    )


def gather_kernel(
    nr, nf, sf_hbm, thr_hbm, codes_hbm, node_hbm, grad_hbm, hess_hbm,
    acc, codes_out, w_out,
    sf_ref, thr_ref, codes_vm, node_vm, grad_vm, hess_vm,
    codes_t, codes_in, codes32, codes_post, flags, child, weight, w, other, below_diagonal,
    load_sem, flag_send, flag_recv, code_send, code_recv, child_send, child_recv,
    weight_send, weight_recv,
):
    rows, feat_dev = codes_vm.shape
    feats = feat_dev // nr
    parents = sf_ref.shape[0]
    nodes = 2 * parents
    my_row, my_feat = lax.axis_index("row"), lax.axis_index("feat")
    group = largest_divisor(feats, 2 * GROUP)

    loads = []
    for i, (source, target) in enumerate(
        (
            (codes_hbm, codes_vm), (sf_hbm, sf_ref), (thr_hbm, thr_ref),
            (node_hbm, node_vm), (grad_hbm, grad_vm), (hess_hbm, hess_vm),
        )
    ):
        load = pltpu.make_async_copy(source, target, load_sem.at[i])
        load.start()
        loads.append(load)
    barrier = pltpu.get_barrier_semaphore()
    for t in range(1, nf):
        pl.semaphore_signal(
            barrier, inc=1, device_id={"feat": lax.rem(my_feat + t, nf)}, device_id_type=MESH
        )
    for t in range(1, nr):
        pl.semaphore_signal(
            barrier, inc=1, device_id={"row": lax.rem(my_row + t, nr)}, device_id_type=MESH
        )

    for load in loads[1:]:
        load.wait()
    parent = lax.broadcasted_iota(jnp.int32, (parents, feat_dev), 0)
    split = jnp.zeros((parents, feat_dev), jnp.int32)
    limit = jnp.zeros((parents, 128), jnp.int32)
    for p in range(parents):
        split = jnp.where(parent == p, sf_ref[p], split)
        limit = jnp.where(parent[:, :128] == p, thr_ref[p], limit)
    column = lax.broadcasted_iota(jnp.int32, (parents, feat_dev), 1) + my_feat * feat_dev
    select = jnp.where(column == split, 1.0, 0.0).astype(BF16)
    loads[0].wait()
    codes = codes_vm[...].astype(F32).astype(BF16)
    picked = lax.dot_general(select, codes, NT, preferred_element_type=F32)
    node = node_vm[...].astype(F32)
    index = lax.broadcasted_iota(jnp.int32, (parents, rows), 0).astype(F32)
    over = (picked > limit[:, :1].astype(F32)) & (node == index)
    flags[0] = jnp.sum(jnp.where(over, 1.0, 0.0), axis=0, keepdims=True)

    eye = (
        lax.broadcasted_iota(jnp.int32, (feat_dev, feat_dev), 0)
        == lax.broadcasted_iota(jnp.int32, (feat_dev, feat_dev), 1)
    )
    eye = jnp.where(eye, 1.0, 0.0).astype(BF16)
    across = lax.dot_general(eye, codes, NT, preferred_element_type=F32)
    codes_t[...] = across.astype(BF16).reshape(nr, feats, rows)

    grad, hess = as_row(grad_vm[...].astype(F32)), as_row(hess_vm[...].astype(F32))
    weight[0, 0:1, :] = grad
    weight[0, 1:2, :] = hess
    early = early_rows(rows)
    half = early // 2
    below_diagonal[...] = jnp.where(
        lax.broadcasted_iota(jnp.int32, (early, early), 0)
        < lax.broadcasted_iota(jnp.int32, (early, early), 1),
        1.0, 0.0,
    ).astype(BF16).astype(FLAG)

    pl.semaphore_wait(barrier, nf + nr - 2)
    flag_copies = []
    for t in range(1, nf):
        copy = pltpu.make_async_remote_copy(
            src_ref=flags.at[0], dst_ref=flags.at[nf - t],
            send_sem=flag_send.at[t - 1], recv_sem=flag_recv.at[t - 1],
            device_id={"feat": lax.rem(my_feat + t, nf)}, device_id_type=MESH,
        )
        copy.start()
        flag_copies.append(copy)

    def to_rows(ref, send, recv):
        copies = []
        for t in range(1, nr):
            copy = pltpu.make_async_remote_copy(
                src_ref=ref.at[0], dst_ref=ref.at[nr - t],
                send_sem=send.at[t - 1], recv_sem=recv.at[t - 1],
                device_id={"row": lax.rem(my_row + t, nr)}, device_id_type=MESH,
            )
            copy.start()
            copies.append(copy)
        return copies

    code_copies = []

    def send_codes(part):
        cut = feats * 3 // 4
        at = pl.ds(cut, feats - cut) if part else pl.ds(0, cut)
        for t in range(1, nr):
            dest = lax.rem(my_row + t, nr)
            copy = pltpu.make_async_remote_copy(
                src_ref=codes_t.at[dest, at], dst_ref=codes_in.at[nr - t - 1, at],
                send_sem=code_send.at[part, t - 1], recv_sem=code_recv.at[part, t - 1],
                device_id={"row": dest}, device_id_type=MESH,
            )
            copy.start()
            code_copies.append(copy)

    send_codes(0)
    weight_copies = to_rows(weight, weight_send, weight_recv)
    codes32[...] = codes_t[my_row].astype(F32)
    after = half + rows - early
    weigh_parents(w, node, grad, hess, early)

    def parents_first(i, carry):
        for j in range(group):
            feature = i * group + j
            acc[feature] = left_sums(w, codes32, feature, 0, early)
        return carry

    lax.fori_loop(0, feats // group, parents_first, 0)
    for copy in flag_copies:
        copy.wait()
    right = jnp.sum(flags[...], axis=0)
    mine = 2.0 * node + right
    child[0] = mine
    child_copies = to_rows(child, child_send, child_recv)
    send_codes(1)

    lines = jnp.concatenate([mine, grad, hess, 2.0 * node + 1.0 - right], axis=0)
    keep_smaller(w, lines, other, codes_post, codes_t.at[my_row], below_diagonal, node, right)
    weigh(w, mine[:, early:], grad[:, early:], hess[:, early:], half)
    codes_post[:, half:] = codes32[:, early:]

    def own_rest(i, carry):
        for j in range(group):
            feature = i * group + j
            part = left_sums(w, codes_post, feature, 0, after)
            acc[feature] = acc[feature] * other[...] + part
        return carry

    lax.fori_loop(0, feats // group, own_rest, 0)

    for t in range(1, nr):
        weight_copies[t - 1].wait()
        child_copies[t - 1].wait()
    for copy in code_copies:
        copy.wait()
    for slot in range(1, nr):
        at = (slot - 1) * rows
        codes_out[:, at : at + rows] = codes_in[slot - 1].astype(F32)
        weigh(w_out, child[slot], weight[slot, 0:1, :], weight[slot, 1:2, :], at)


def gain_kernel(rows, acc, codes32, w, out_hbm, out_vm, more_sums, out_sem):
    feats, others = codes32.shape[0], codes32.shape[1] // rows
    nodes = w.shape[0] // 2
    group = largest_divisor(feats, 4 * GROUP)
    step_out = largest_divisor(group, 2)
    span = largest_divisor(others, 3)
    width = span * rows
    middle = others // span - 1

    def more(step, carry):
        start = pl.multiple_of(step * width, rows)

        def some(i, inner):
            for j in range(group):
                feature = i * group + j
                part = left_sums(w, codes32, feature, start, width)
                more_sums[feature] += part
            return inner

        return lax.fori_loop(0, feats // group, some, carry)

    if middle:
        more_sums[...] = jnp.zeros(more_sums.shape, F32)
        lax.fori_loop(0, middle, more, 0)

    def last(i, carry):
        for j in range(group):
            feature = i * group + j
            left = acc[feature] + left_sums(w, codes32, feature, middle * width, width)
            if middle:
                left = left + more_sums[feature]
            grad_left, hess_left = left[:nodes], left[nodes:]
            grad_all, hess_all = grad_left[:, BINS - 1 :], hess_left[:, BINS - 1 :]
            grad_right, hess_right = grad_all - grad_left, hess_all - hess_left
            value = grad_left * grad_left / (hess_left + 1.0)
            value += grad_right * grad_right / (hess_right + 1.0)
            out_vm[feature] = 0.5 * (value - grad_all * grad_all / (hess_all + 1.0))
            if (j + 1) % step_out == 0:
                at = pl.ds(feature + 1 - step_out, step_out)
                pltpu.make_async_copy(out_vm.at[at], out_hbm.at[at], out_sem).start()
        return carry

    lax.fori_loop(0, feats // group, last, 0)
    pltpu.make_async_copy(out_vm, out_hbm, out_sem).wait()


def local(nr, nf, codes, node_ids, grads, hessians, split_feature, threshold):
    rows, feat_dev = codes.shape
    feats = feat_dev // nr
    parents = split_feature.shape[0]
    nodes = 2 * parents
    others = (nr - 1) * rows
    middle = (nr - 1) // largest_divisor(nr - 1, 3) - 1
    early = early_rows(rows)
    vmem, smem = pltpu.VMEM, pltpu.SMEM
    dma = pltpu.SemaphoreType.DMA
    in_vmem, in_hbm = pl.BlockSpec(memory_space=vmem), pl.BlockSpec(memory_space=pltpu.HBM)
    block = (rows // 128, 128)
    acc, codes32, w = pl.pallas_call(
        functools.partial(gather_kernel, nr, nf),
        out_shape=(
            jax.ShapeDtypeStruct((feats, 2 * nodes, BINS), F32),
            jax.ShapeDtypeStruct((feats, others), F32),
            jax.ShapeDtypeStruct((2 * nodes, others), BF16),
        ),
        in_specs=[in_hbm] * 6,
        out_specs=(in_vmem, in_vmem, in_vmem),
        scratch_shapes=[
            smem((parents,), jnp.int32),
            smem((parents,), jnp.int32),
            vmem((rows, feat_dev), jnp.int32),
            vmem((1, rows), jnp.int32),
            vmem(block, BF16),
            vmem(block, BF16),
            vmem((nr, feats, rows), BF16),
            vmem((nr - 1, feats, rows), BF16),
            vmem((feats, rows), F32),
            vmem((feats, rows - early + early // 2), F32),
            vmem((nf, 1, rows), F32),
            vmem((nr, 1, rows), F32),
            vmem((nr, 2, rows), F32),
            vmem((2 * nodes, rows), BF16),
            vmem((2 * nodes, BINS), F32),
            vmem((early, early), FLAG),
            dma((6,)),
            dma((nf - 1,)),
            dma((nf - 1,)),
            dma((2, nr - 1)),
            dma((2, nr - 1)),
            dma((nr - 1,)),
            dma((nr - 1,)),
            dma((nr - 1,)),
            dma((nr - 1,)),
        ],
        compiler_params=pltpu.CompilerParams(
            collective_id=0, has_side_effects=True, vmem_limit_bytes=32 << 20
        ),
    )(
        *(
            pltpu.with_memory_space_constraint(x, pltpu.HBM)
            for x in (
                split_feature, threshold, codes, node_ids.reshape(1, rows),
                grads.reshape(block), hessians.reshape(block),
            )
        )
    )
    return pl.pallas_call(
        functools.partial(gain_kernel, rows),
        out_shape=jax.ShapeDtypeStruct((feats, nodes, BINS), F32),
        in_specs=[in_vmem] * 3,
        out_specs=in_hbm,
        scratch_shapes=[
            vmem((feats, nodes, BINS), F32),
            vmem((feats if middle else 1, 2 * nodes, BINS), F32),
            dma,
        ],
        compiler_params=pltpu.CompilerParams(vmem_limit_bytes=32 << 20),
    )(acc, codes32, w)


def solution(mesh):
    return jax.shard_map(
        functools.partial(local, mesh.shape["row"], mesh.shape["feat"]),
        mesh=mesh,
        in_specs=(P("row", "feat"), P("row"), P("row"), P("row"), P(), P()),
        out_specs=P(("feat", "row"), None, None),
        check_vma=False,
    )
```

```python
import functools

import jax
import jax.numpy as jnp
from jax import lax
from jax.experimental import pallas as pl
from jax.experimental.pallas import tpu as pltpu
from jax.sharding import PartitionSpec as P

BINS = 256
GROUP = 16
MESH = pl.DeviceIdType.MESH
NT = (((1,), (1,)), ((), ()))
F32, BF16, FLAG = jnp.float32, jnp.bfloat16, jnp.float8_e4m3fn


def largest_divisor(number, limit):
    return max(d for d in range(1, limit + 1) if number % d == 0)


def as_row(block):
    return jnp.concatenate([block[i : i + 1] for i in range(block.shape[0])], axis=1)


def weigh(w, child, grad, hess, start):
    nodes, width = w.shape[0] // 2, child.shape[1]
    number = lax.broadcasted_iota(jnp.int32, (nodes, width), 0).astype(F32)
    member = child == number
    w[0:nodes, start : start + width] = jnp.where(member, grad, 0.0).astype(BF16)
    w[nodes:, start : start + width] = jnp.where(member, hess, 0.0).astype(BF16)


def weigh_parents(w, node, grad, hess, width):
    nodes = w.shape[0] // 2
    member = node[:, :width] == parent_number(nodes, width)
    w[0:nodes, 0:width] = jnp.where(member, grad[:, :width], 0.0).astype(BF16)
    w[nodes:, 0:width] = jnp.where(member, hess[:, :width], 0.0).astype(BF16)


def parent_number(nodes, width):
    return (lax.broadcasted_iota(jnp.int32, (nodes, width), 0) // 2).astype(F32)


def early_rows(rows):
    return rows // 2


def keep_smaller(w, lines, other, codes_post, codes_own, below_diagonal, node, right):
    nodes, early = w.shape[0] // 2, below_diagonal.shape[0]
    half = early // 2
    bit = right[:, :early]
    member = node[:, :early] == parent_number(nodes, early)
    in_all = jnp.sum(jnp.where(member, 1.0, 0.0), axis=1, keepdims=True)
    in_right = jnp.sum(jnp.where(member, bit, 0.0), axis=1, keepdims=True)
    side = jnp.where(2.0 * in_right <= in_all, 1.0, 0.0)
    odd = lax.broadcasted_iota(jnp.int32, (nodes, 1), 0) % 2
    larger = jnp.where(odd.astype(F32) == side, 0.0, 1.0)
    other[0:nodes] = jnp.broadcast_to(larger, (nodes, other.shape[1]))
    other[nodes:] = jnp.broadcast_to(larger, (nodes, other.shape[1]))
    side_row = 0.5 * jnp.sum(jnp.where(member, side, 0.0), axis=0, keepdims=True)
    chosen = bit == side_row
    ones = jnp.broadcast_to(jnp.where(chosen, 1.0, 0.0), (16, early)).astype(BF16)
    rank = jnp.dot(ones, below_diagonal[...], preferred_element_type=F32)[0:1]
    rank = jnp.where(chosen, rank, -1.0)
    place = lax.broadcasted_iota(jnp.int32, (half, early), 0).astype(F32)
    move = jnp.where(rank == place, 1.0, 0.0).astype(BF16).astype(FLAG)
    lines = lax.dot_general(
        lines[:, :early].astype(BF16), move, NT, preferred_element_type=F32
    )
    codes_post[:, 0:half] = lax.dot_general(
        codes_own[:, 0:early], move, NT, preferred_element_type=F32
    )
    number = lax.broadcasted_iota(jnp.int32, (nodes, half), 0).astype(F32)
    plus, minus = lines[0:1] == number, lines[3:4] == number
    for k in range(2):
        value = lines[k + 1 : k + 2]
        value = jnp.where(plus, value, jnp.where(minus, -value, 0.0))
        w[k * nodes : (k + 1) * nodes, 0:half] = value.astype(BF16)


def below(codes32, feature, start, width):
    code = codes32[pl.ds(feature, 1), pl.ds(start, width)].astype(BF16)
    bins = lax.broadcasted_iota(jnp.int32, (BINS, width), 0).astype(F32).astype(BF16)
    one, zero = jnp.ones((), FLAG), jnp.zeros((), FLAG)
    return jnp.where(bins >= code, one, zero)


def left_sums(w, codes32, feature, start, width):
    return lax.dot_general(
        w[:, pl.ds(start, width)], below(codes32, feature, start, width), NT,
        preferred_element_type=F32,
    )


def gather_kernel(
    nr, nf, sf_hbm, thr_hbm, codes_hbm, node_hbm, grad_hbm, hess_hbm,
    acc, codes_out, w_out,
    sf_ref, thr_ref, codes_vm, node_vm, grad_vm, hess_vm,
    codes_t, codes_in, codes32, codes_post, flags, child, weight, w, other, below_diagonal,
    load_sem, flag_send, flag_recv, code_send, code_recv, child_send, child_recv,
    weight_send, weight_recv,
):
    rows, feat_dev = codes_vm.shape
    feats = feat_dev // nr
    parents = sf_ref.shape[0]
    nodes = 2 * parents
    my_row, my_feat = lax.axis_index("row"), lax.axis_index("feat")
    group = largest_divisor(feats, 2 * GROUP)

    loads = []
    for i, (source, target) in enumerate(
        (
            (codes_hbm, codes_vm), (sf_hbm, sf_ref), (thr_hbm, thr_ref),
            (node_hbm, node_vm), (grad_hbm, grad_vm), (hess_hbm, hess_vm),
        )
    ):
        load = pltpu.make_async_copy(source, target, load_sem.at[i])
        load.start()
        loads.append(load)
    barrier = pltpu.get_barrier_semaphore()
    for t in range(1, nf):
        pl.semaphore_signal(
            barrier, inc=1, device_id={"feat": lax.rem(my_feat + t, nf)}, device_id_type=MESH
        )
    for t in range(1, nr):
        pl.semaphore_signal(
            barrier, inc=1, device_id={"row": lax.rem(my_row + t, nr)}, device_id_type=MESH
        )

    for load in loads[1:]:
        load.wait()
    parent = lax.broadcasted_iota(jnp.int32, (parents, feat_dev), 0)
    split = jnp.zeros((parents, feat_dev), jnp.int32)
    limit = jnp.zeros((parents, 128), jnp.int32)
    for p in range(parents):
        split = jnp.where(parent == p, sf_ref[p], split)
        limit = jnp.where(parent[:, :128] == p, thr_ref[p], limit)
    column = lax.broadcasted_iota(jnp.int32, (parents, feat_dev), 1) + my_feat * feat_dev
    select = jnp.where(column == split, 1.0, 0.0).astype(BF16)
    loads[0].wait()
    codes = codes_vm[...].astype(F32).astype(BF16)
    picked = lax.dot_general(select, codes, NT, preferred_element_type=F32)
    node = node_vm[...].astype(F32)
    index = lax.broadcasted_iota(jnp.int32, (parents, rows), 0).astype(F32)
    over = (picked > limit[:, :1].astype(F32)) & (node == index)
    flags[0] = jnp.sum(jnp.where(over, 1.0, 0.0), axis=0, keepdims=True)

    eye = (
        lax.broadcasted_iota(jnp.int32, (feat_dev, feat_dev), 0)
        == lax.broadcasted_iota(jnp.int32, (feat_dev, feat_dev), 1)
    )
    eye = jnp.where(eye, 1.0, 0.0).astype(BF16)
    across = lax.dot_general(eye, codes, NT, preferred_element_type=F32)
    codes_t[...] = across.astype(BF16).reshape(nr, feats, rows)

    grad, hess = as_row(grad_vm[...].astype(F32)), as_row(hess_vm[...].astype(F32))
    weight[0, 0:1, :] = grad
    weight[0, 1:2, :] = hess
    early = early_rows(rows)
    half = early // 2
    below_diagonal[...] = jnp.where(
        lax.broadcasted_iota(jnp.int32, (early, early), 0)
        < lax.broadcasted_iota(jnp.int32, (early, early), 1),
        1.0, 0.0,
    ).astype(BF16).astype(FLAG)

    pl.semaphore_wait(barrier, nf + nr - 2)
    flag_copies = []
    for t in range(1, nf):
        copy = pltpu.make_async_remote_copy(
            src_ref=flags.at[0], dst_ref=flags.at[nf - t],
            send_sem=flag_send.at[t - 1], recv_sem=flag_recv.at[t - 1],
            device_id={"feat": lax.rem(my_feat + t, nf)}, device_id_type=MESH,
        )
        copy.start()
        flag_copies.append(copy)

    def to_rows(ref, send, recv):
        copies = []
        for t in range(1, nr):
            copy = pltpu.make_async_remote_copy(
                src_ref=ref.at[0], dst_ref=ref.at[nr - t],
                send_sem=send.at[t - 1], recv_sem=recv.at[t - 1],
                device_id={"row": lax.rem(my_row + t, nr)}, device_id_type=MESH,
            )
            copy.start()
            copies.append(copy)
        return copies

    code_copies = []

    def send_codes(part):
        cut = feats // 32 * 16 or feats
        size = feats - cut if part else cut
        if not size:
            return
        at = pl.ds(part * cut, size)
        for t in range(1, nr):
            dest = lax.rem(my_row + t, nr)
            copy = pltpu.make_async_remote_copy(
                src_ref=codes_t.at[dest, at], dst_ref=codes_in.at[nr - t - 1, at],
                send_sem=code_send.at[part, t - 1], recv_sem=code_recv.at[part, t - 1],
                device_id={"row": dest}, device_id_type=MESH,
            )
            copy.start()
            code_copies.append(copy)

    send_codes(0)
    weight_copies = to_rows(weight, weight_send, weight_recv)
    codes32[...] = codes_t[my_row].astype(F32)
    after = half + rows - early
    weigh_parents(w, node, grad, hess, early)

    def parents_first(i, carry):
        for j in range(group):
            feature = i * group + j
            acc[feature] = left_sums(w, codes32, feature, 0, early)
        return carry

    lax.fori_loop(0, feats // group, parents_first, 0)
    for copy in flag_copies:
        copy.wait()
    right = jnp.sum(flags[...], axis=0)
    mine = 2.0 * node + right
    child[0] = mine
    child_copies = to_rows(child, child_send, child_recv)
    send_codes(1)

    lines = jnp.concatenate([mine, grad, hess, 2.0 * node + 1.0 - right], axis=0)
    keep_smaller(w, lines, other, codes_post, codes_t.at[my_row], below_diagonal, node, right)
    weigh(w, mine[:, early:], grad[:, early:], hess[:, early:], half)
    codes_post[:, half:] = codes32[:, early:]

    def own_rest(i, carry):
        for j in range(group):
            feature = i * group + j
            part = left_sums(w, codes_post, feature, 0, after)
            acc[feature] = acc[feature] * other[...] + part
        return carry

    lax.fori_loop(0, feats // group, own_rest, 0)

    for t in range(1, nr):
        weight_copies[t - 1].wait()
        child_copies[t - 1].wait()
    for copy in code_copies:
        copy.wait()
    for slot in range(1, nr):
        at = (slot - 1) * rows
        codes_out[:, at : at + rows] = codes_in[slot - 1].astype(F32)
        weigh(w_out, child[slot], weight[slot, 0:1, :], weight[slot, 1:2, :], at)


def gain_kernel(rows, acc, codes32, w, out_hbm, out_vm, more_sums, out_sem):
    feats, others = codes32.shape[0], codes32.shape[1] // rows
    nodes = w.shape[0] // 2
    group = largest_divisor(feats, 4 * GROUP)
    step_out = largest_divisor(group, 2)
    span = largest_divisor(others, 3)
    width = span * rows
    middle = others // span - 1

    def more(step, carry):
        start = pl.multiple_of(step * width, rows)

        def some(i, inner):
            for j in range(group):
                feature = i * group + j
                part = left_sums(w, codes32, feature, start, width)
                more_sums[feature] += part
            return inner

        return lax.fori_loop(0, feats // group, some, carry)

    if middle:
        more_sums[...] = jnp.zeros(more_sums.shape, F32)
        lax.fori_loop(0, middle, more, 0)

    def last(i, carry):
        for j in range(group):
            feature = i * group + j
            left = acc[feature] + left_sums(w, codes32, feature, middle * width, width)
            if middle:
                left = left + more_sums[feature]
            grad_left, hess_left = left[:nodes], left[nodes:]
            grad_all, hess_all = grad_left[:, BINS - 1 :], hess_left[:, BINS - 1 :]
            grad_right, hess_right = grad_all - grad_left, hess_all - hess_left
            value = grad_left * grad_left / (hess_left + 1.0)
            value += grad_right * grad_right / (hess_right + 1.0)
            out_vm[feature] = 0.5 * (value - grad_all * grad_all / (hess_all + 1.0))
            if (j + 1) % step_out == 0:
                at = pl.ds(feature + 1 - step_out, step_out)
                pltpu.make_async_copy(out_vm.at[at], out_hbm.at[at], out_sem).start()
        return carry

    lax.fori_loop(0, feats // group, last, 0)
    pltpu.make_async_copy(out_vm, out_hbm, out_sem).wait()


def local(nr, nf, codes, node_ids, grads, hessians, split_feature, threshold):
    rows, feat_dev = codes.shape
    feats = feat_dev // nr
    parents = split_feature.shape[0]
    nodes = 2 * parents
    others = (nr - 1) * rows
    middle = (nr - 1) // largest_divisor(nr - 1, 3) - 1
    early = early_rows(rows)
    vmem, smem = pltpu.VMEM, pltpu.SMEM
    dma = pltpu.SemaphoreType.DMA
    in_vmem, in_hbm = pl.BlockSpec(memory_space=vmem), pl.BlockSpec(memory_space=pltpu.HBM)
    block = (rows // 128, 128)
    acc, codes32, w = pl.pallas_call(
        functools.partial(gather_kernel, nr, nf),
        out_shape=(
            jax.ShapeDtypeStruct((feats, 2 * nodes, BINS), F32),
            jax.ShapeDtypeStruct((feats, others), F32),
            jax.ShapeDtypeStruct((2 * nodes, others), BF16),
        ),
        in_specs=[in_hbm] * 6,
        out_specs=(in_vmem, in_vmem, in_vmem),
        scratch_shapes=[
            smem((parents,), jnp.int32),
            smem((parents,), jnp.int32),
            vmem((rows, feat_dev), jnp.int32),
            vmem((1, rows), jnp.int32),
            vmem(block, BF16),
            vmem(block, BF16),
            vmem((nr, feats, rows), BF16),
            vmem((nr - 1, feats, rows), BF16),
            vmem((feats, rows), F32),
            vmem((feats, rows - early + early // 2), F32),
            vmem((nf, 1, rows), F32),
            vmem((nr, 1, rows), F32),
            vmem((nr, 2, rows), F32),
            vmem((2 * nodes, rows), BF16),
            vmem((2 * nodes, BINS), F32),
            vmem((early, early), FLAG),
            dma((6,)),
            dma((nf - 1,)),
            dma((nf - 1,)),
            dma((2, nr - 1)),
            dma((2, nr - 1)),
            dma((nr - 1,)),
            dma((nr - 1,)),
            dma((nr - 1,)),
            dma((nr - 1,)),
        ],
        compiler_params=pltpu.CompilerParams(
            collective_id=0, has_side_effects=True, vmem_limit_bytes=32 << 20
        ),
    )(
        *(
            pltpu.with_memory_space_constraint(x, pltpu.HBM)
            for x in (
                split_feature, threshold, codes, node_ids.reshape(1, rows),
                grads.reshape(block), hessians.reshape(block),
            )
        )
    )
    return pl.pallas_call(
        functools.partial(gain_kernel, rows),
        out_shape=jax.ShapeDtypeStruct((feats, nodes, BINS), F32),
        in_specs=[in_vmem] * 3,
        out_specs=in_hbm,
        scratch_shapes=[
            vmem((feats, nodes, BINS), F32),
            vmem((feats if middle else 1, 2 * nodes, BINS), F32),
            dma,
        ],
        compiler_params=pltpu.CompilerParams(vmem_limit_bytes=32 << 20),
    )(acc, codes32, w)


def solution(mesh):
    return jax.shard_map(
        functools.partial(local, mesh.shape["row"], mesh.shape["feat"]),
        mesh=mesh,
        in_specs=(P("row", "feat"), P("row"), P("row"), P("row"), P(), P()),
        out_specs=P(("feat", "row"), None, None),
        check_vma=False,
    )
```
